256 devices in a mesh: row: 4 (over z_hi), col: 64 (over x, y, z_lo, core).
Axes of the slice: x: 4, y: 4, z: 8 (z_hi: 4, z_lo: 2; z = z_hi * 2 + z_lo), core: 2. Of those that a mesh axis runs over, the one named last changes fastest.
Arguments:
- src_emb: bfloat16 [32768, 256], P(('row', 'col')), may hold values from -64 to 64
- dst_emb: bfloat16 [32768, 256], P('col'), may hold values from -64 to 64
- state_emb: bfloat16 [32768, 256], P('col'), may hold values from -64 to 64
- word_emb: bfloat16 [32000, 256], P('row'), may hold values from -64 to 64
- start_probs: bfloat16 [64, 32768], P(None, 'row'), may hold values from 0.099609375 to 10
- token_ids: int32 [64, 2], replicated, may hold values from 0 to 31999
Outputs:
- final_probs: float32 [64, 32768], P(None, 'col')
- log_norm: float32 [64], replicated
The draws below stay inside these ranges and needn't reach their ends.
All inputs are finite; a program needn't handle non-finite values.
Results may differ from the reference program's by a relative error of at most 0.0003.
The reference program's roundings to bfloat16 on the way count: a program that leaves them out, or rounds other values in their place, can miss the bound.
Values may be sent and summed in bfloat16 or wider, within the bound.
A program may use at most 128 MiB of HBM per device.

```python
import math
import jax
import jax.numpy as jnp
import numpy as np
from jax import lax

S = 32768
E = 256
V = 32000
B = 64
STEPS = 2


def drawn_pair(key, first_rows, second_rows):
    keys = jax.random.split(key, 2)
    spread = (3.0 / math.sqrt(E)) ** 0.5
    first = jnp.clip(jax.random.normal(keys[0], (first_rows, E), jnp.float32), -5.0, 5.0) * spread
    second = jnp.clip(jax.random.normal(keys[1], (second_rows, E), jnp.float32), -5.0, 5.0) * spread
    return (first, second)


def draw_src_emb(key, part):
    return drawn_pair(jax.random.fold_in(key, 11), S, S)[0].astype(jnp.bfloat16)


def draw_dst_emb(key, part):
    return drawn_pair(jax.random.fold_in(key, 11), S, S)[1].astype(jnp.bfloat16)


def draw_state_emb(key, part):
    return drawn_pair(jax.random.fold_in(key, 23), S, V)[0].astype(jnp.bfloat16)


def draw_word_emb(key, part):
    return drawn_pair(jax.random.fold_in(key, 23), S, V)[1].astype(jnp.bfloat16)


def plant(array, stream_key, low, high):
    extent = array.shape
    index_at = [jax.random.randint(jax.random.fold_in(stream_key, axis), (), 0, extent[axis]) for axis in range(len(extent))]
    array = array.at[tuple(index_at)].set(low)
    longest = extent.index(max(extent))
    index_at[longest] = (index_at[longest] + 1) % extent[longest]
    return array.at[tuple(index_at)].set(high)


def steps_of(key, extent, cuts, smallest, top_value):
    def one(axis_at, parts):
        steps = jax.random.uniform(jax.random.fold_in(jax.random.fold_in(key, 6), axis_at), (parts,), jnp.float32, smallest / len(cuts), top_value / len(cuts))
        return jnp.repeat(jnp.exp(steps), extent[axis_at] // parts).reshape((-1,) + (1,) * (len(extent) - axis_at - 1))

    gain = one(*cuts[0])
    for cut in cuts[1:]:
        gain = gain * one(*cut)
    return gain


def cumulative_ranks(count, slope):
    loads = [(1 << 20) // math.isqrt(rank ** slope) + 1 for rank in range(1, count + 1)]
    width = 1 + sum(loads) // (1 << 30)
    return np.cumsum(np.array([max(1, weight // width) for weight in loads]))


def skewed_ids(stream_key, shape, amount, skew):
    listing = cumulative_ranks(amount, skew)
    pick = jax.random.randint(jax.random.fold_in(stream_key, 1), shape, 0, int(listing[amount - 1]))
    standing = jnp.searchsorted(jnp.asarray(listing, jnp.int32), pick, side="right")
    return jax.random.permutation(jax.random.fold_in(stream_key, 2), amount)[standing].astype(jnp.int32)


def setup_inputs(seed: int = 0) -> dict:
    key_of = jax.random.split(jax.random.key(seed), 7)
    src_emb = draw_src_emb(jax.random.fold_in(key_of[6], 71), 0)
    dst_emb = draw_dst_emb(jax.random.fold_in(key_of[6], 71), 0)
    state_emb = draw_state_emb(jax.random.fold_in(key_of[6], 71), 0)
    word_emb = draw_word_emb(jax.random.fold_in(key_of[6], 71), 0)
    start_probs = jnp.clip(jnp.exp(math.log(10.0) - 4.609084 * jax.random.uniform(key_of[4], (B, S), jnp.float32) ** steps_of(key_of[4], (B, S), ((1, 4),), -0.2, 0.2)), 0.099609375, 10.0).astype(jnp.bfloat16)
    token_ids = plant(skewed_ids(key_of[5], (B, STEPS), V, 2), jax.random.fold_in(key_of[5], 3), 0, V - 1).astype(jnp.int32)
    return dict(src_emb=src_emb, dst_emb=dst_emb, state_emb=state_emb, word_emb=word_emb, start_probs=start_probs, token_ids=token_ids)


def reference(src_emb, dst_emb, state_emb, word_emb, start_probs, token_ids):
    block_rows = math.gcd(S, 1024)
    block_count = S // block_rows

    def vocab_block(rows):
        logits = jnp.dot(rows, word_emb.T, preferred_element_type=jnp.float32)
        top = jnp.max(logits, axis=1)
        return top + jnp.log(jnp.sum(jnp.exp(logits - top[:, None]), axis=1))

    state_norm = lax.map(vocab_block, state_emb.reshape(block_count, block_rows, E)).reshape(S)
    token_vecs = word_emb[token_ids.reshape(-1)]
    scores = jnp.dot(token_vecs, state_emb.T, preferred_element_type=jnp.float32)
    emit = jnp.exp(scores - state_norm[None, :]).reshape(B, STEPS, S)

    def advance(probs):
        def one_block(total, index):
            start = (index * block_rows).astype(jnp.int32)
            rows = lax.dynamic_slice_in_dim(src_emb, start, block_rows, 0)
            logits = jnp.dot(rows, dst_emb.T, preferred_element_type=jnp.float32)
            top = jnp.max(logits, axis=1)
            shifted = jnp.exp(logits - top[:, None])
            row_total = jnp.sum(shifted, axis=1)
            trans = shifted.astype(jnp.bfloat16)
            part = lax.dynamic_slice_in_dim(probs, start, block_rows, 1).astype(jnp.float32)
            weights = (part / row_total[None, :]).astype(jnp.bfloat16)
            return total + jnp.dot(weights, trans, preferred_element_type=jnp.float32), None

        result, _ = lax.scan(one_block, jnp.zeros((B, S), jnp.float32), jnp.arange(block_count, dtype=jnp.int32))
        return result

    joint1 = advance(start_probs) * emit[:, 0]
    scale1 = jnp.sum(joint1, axis=1) / S
    probs1 = (joint1 / scale1[:, None]).astype(jnp.bfloat16)
    joint2 = advance(probs1) * emit[:, 1]
    scale2 = jnp.sum(joint2, axis=1) / S
    final_probs = joint2 / scale2[:, None]
    log_norm = jnp.log(scale1) + jnp.log(scale2)
    return final_probs, log_norm
```

```python
import functools

import jax
import jax.numpy as jnp
from jax import lax
from jax.experimental import pallas as pl
from jax.experimental.pallas import tpu as pltpu
from jax.sharding import PartitionSpec as P

S = 32768
E = 256
B = 64
ROWS = 4
PLANE = 16
ZK = 4
NC = 2048
BLK = 128
WCH = 800
MESH = pl.DeviceIdType.MESH
F32 = jnp.float32
BF16 = jnp.bfloat16
NT = (((1,), (1,)), ((), ()))


def al(value, step):
    return pl.multiple_of(value, step)


def kernel(
    ids_ref, src_ref, dst_ref, state_ref, word_ref, sp_ref, out_ref, ln_ref,
    word_v, state_v, dst_v, src_v, sp_v, p_v, t_v, w_v, tok_v, acc_v, vst_r, st_r, stat_v,
    emit_v, part_v, cs_s, cs_r, zs_s, zs_r, j_v, col_r, pl_r, fin_v,
    loc_sem, pi_s, pi_r, dst_s, dst_r, ag_s, ag_r, sp_s, sp_r, tok_s, tok_r, vst_ss, vst_rs, st_ss, st_rs,
    cs_ss, cs_rs, zs_ss, zs_rs, j_ss, j_rs, col_ss, col_rs, pl_ss, pl_rs, fin_ss, fin_rs,
):
    r = lax.axis_index("row")
    c = lax.axis_index("col")
    n = c // 4
    x = n // 4
    y = n % 4
    zk = c % 4
    zl = zk // 2
    k = zk % 2
    q = r * 4 + zk

    def send(src, dst, ss, rs, row, col):
        return pltpu.make_async_remote_copy(
            src_ref=src, dst_ref=dst, send_sem=ss, recv_sem=rs,
            device_id=(row, col), device_id_type=MESH,
        )

    def plane(d):
        return lax.rem(n + d, PLANE)

    def column(d):
        return lax.rem(q + d, PLANE)

    my_state = state_v.at[pl.ds(al(zl * 512, 512), 512), :]
    cp_state = pltpu.make_async_copy(state_ref, my_state, loc_sem.at[0])
    cp_state.start()
    cp_word = pltpu.make_async_copy(word_ref, word_v, loc_sem.at[1])
    cp_word.start()
    cp_dst = pltpu.make_async_copy(dst_ref, dst_v.at[pl.ds(al(zk * 512, 512), 512), :], loc_sem.at[2])
    cp_dst.start()

    rt = c % 4
    ct = r * 16 + c // 4
    rf = c // 16
    cf = (c % 16) * 4 + r
    moved = jnp.logical_or(rt != r, ct != c)

    barrier = pltpu.get_barrier_semaphore()

    @pl.loop(1, PLANE)
    def _(d):
        pl.semaphore_signal(barrier, inc=1, device_id=(r, plane(d) * 4 + zk), device_id_type=MESH)
        other = column(d)
        pl.semaphore_signal(
            barrier, inc=1, device_id=(other // 4, n * 4 + other % 4), device_id_type=MESH
        )

    @pl.when(moved)
    def _():
        pl.semaphore_signal(barrier, inc=1, device_id=(rt, ct), device_id_type=MESH)
        pl.semaphore_signal(barrier, inc=1, device_id=(rf, cf), device_id_type=MESH)

    cp_state.wait()
    cp_word.wait()
    acc_v[...] = jnp.zeros_like(acc_v)
    base = r * 8000

    def vocab(i, carry):
        m, s = carry
        words = word_v[pl.ds(al(i * WCH, 16), WCH), :]
        l = lax.dot_general(words, my_state[...], NT, preferred_element_type=F32)
        m2 = jnp.maximum(m, jnp.max(l, axis=0, keepdims=True))
        s2 = s * jnp.exp(m - m2) + jnp.sum(jnp.exp(l - m2), axis=0, keepdims=True)
        at = lax.broadcasted_iota(jnp.int32, (B, WCH), 1) + (base + i * WCH)
        for t in range(2):
            hot = jnp.where(ids_ref[:, t:t + 1] == at, 1.0, 0.0).astype(BF16)
            acc_v[t * B:(t + 1) * B, :] += jnp.dot(hot, words, preferred_element_type=F32)
        return m2, s2

    init = (jnp.full((1, 512), -jnp.inf, F32), jnp.zeros((1, 512), F32))
    carry = lax.fori_loop(0, 4, vocab, init)

    pl.semaphore_wait(barrier, jnp.where(moved, 32, 30))

    nt = ct // 4
    sp_mine = sp_ref.at[:, pl.ds(al(c * BLK, BLK), BLK)]
    my_rows = src_v.at[pl.ds(al(n * BLK, BLK), BLK), :]
    my_sp = sp_v.at[pl.ds(al(n * B, B), B), :]
    pi_src = send(src_ref, src_v.at[pl.ds(al(nt * BLK, BLK), BLK), :], pi_s.at[0], pi_r.at[0], rt, ct)
    pi_sp = send(sp_mine, sp_v.at[pl.ds(al(nt * B, B), B), :], pi_s.at[1], pi_r.at[1], rt, ct)

    @pl.when(moved)
    def _():
        pi_src.start()
        pi_sp.start()

    @pl.when(jnp.logical_not(moved))
    def _():
        a = pltpu.make_async_copy(src_ref, my_rows, loc_sem.at[3])
        b = pltpu.make_async_copy(sp_mine, my_sp, loc_sem.at[4])
        a.start()
        b.start()
        a.wait()
        b.wait()

    z = r * 2 + zl
    up = lax.rem(z + 1, 8)
    down = lax.rem(z + 7, 8)
    dst_core = send(
        dst_ref, dst_v.at[pl.ds(al(zk * 512, 512), 512), :], dst_s.at[4], dst_r.at[4],
        r, n * 4 + zl * 2 + (1 - k),
    )
    dst_core.start()
    dst_copies = []
    for half, to in ((0, up), (1, down)):
        for kt in range(2):
            cpy = send(
                dst_ref.at[pl.ds(half * 256, 256), :],
                dst_v.at[pl.ds(al(zk * 512 + half * 256, 256), 256), :],
                dst_s.at[half * 2 + kt], dst_r.at[half * 2 + k],
                to // 2, n * 4 + (to % 2) * 2 + kt,
            )
            cpy.start()
            dst_copies.append(cpy)
        cpy = send(
            state_ref.at[pl.ds(half * 256, 256), :],
            state_v.at[pl.ds(al(zl * 512 + half * 256, 256), 256), :],
            dst_s.at[5 + half], dst_r.at[5 + half],
            to // 2, n * 4 + (to % 2) * 2 + k,
        )
        cpy.start()
        dst_copies.append(cpy)

    carry = lax.fori_loop(4, 7, vocab, carry)

    @pl.when(moved)
    def _():
        send(src_ref, my_rows, pi_s.at[0], pi_r.at[0], rf, cf).wait_recv()
        send(sp_mine, my_sp, pi_s.at[1], pi_r.at[1], rf, cf).wait_recv()

    def half_of(slot, half):
        return src_v.at[pl.ds(al(slot * BLK + half * 64, 64), 64), :]

    def pass_on(slot, half, ss, xt, yt):
        ref = half_of(slot, half)
        return send(
            ref, ref, ag_s.at[ss], ag_r.at[half * PLANE + slot], r, (xt * 4 + yt) * 4 + zk
        )

    def own_copy(part, d):
        half = part % 2
        if part in (0, 3):
            return pass_on(n, half, part * 4 + d, (x + d) % 4, y)
        return pass_on(n, half, part * 4 + d, x, (y + d) % 4)

    def forward(half, d, e):
        if half == 0:
            return pass_on((x + d) % 4 * 4 + y, 0, 16 + d * 4 + e, x, (y + e) % 4)
        return pass_on(x * 4 + (y + d) % 4, 1, 32 + d * 4 + e, (x + e) % 4, y)

    for part in range(4):
        for d in (1, 3, 2):
            own_copy(part, d).start()

    vm, vs = lax.fori_loop(7, 10, vocab, carry)

    me = zl * 4 + r
    my_vst = vst_r.at[me]
    my_vst[0:1, :] = vm
    my_vst[1:2, :] = vs
    tok_mine = tok_v.at[pl.ds(al(r * 128, 128), 128), :]
    tok_mine[...] = acc_v[...].astype(BF16)

    def vst_copy(d, at):
        to = lax.rem(me + d, 8)
        ref = vst_r.at[at]
        return send(
            ref, ref, vst_ss.at[d], vst_rs.at[at], to % 4, n * 4 + (to // 4) * 2 + k
        )

    for d in (1, 3, 2):
        pass_on((x + d) % 4 * 4 + y, 0, d, x, y).wait_recv()
        for e in (1, 3, 2):
            forward(0, d, e).start()
        pass_on(x * 4 + (y + d) % 4, 1, 4 + d, x, y).wait_recv()
        for e in (1, 3, 2):
            forward(1, d, e).start()

    @pl.loop(1, PLANE)
    def _(d):
        send(my_sp, my_sp, sp_s.at[d], sp_r.at[n], r, plane(d) * 4 + zk).start()

    @pl.loop(1, 8)
    def _(d):
        vst_copy(d, me).start()

    @pl.loop(1, ROWS)
    def _(d):
        send(tok_mine, tok_mine, tok_s.at[d], tok_r.at[r], lax.rem(r + d, ROWS), c).start()

    cp_dst.wait()
    send(
        dst_ref, dst_v.at[pl.ds(al((zl * 2 + 1 - k) * 512, 512), 512), :], dst_s.at[4], dst_r.at[4],
        r, n * 4 + zl * 2 + (1 - k),
    ).wait_recv()
    for half in range(2):
        for kf in range(2):
            send(
                dst_ref.at[pl.ds(half * 256, 256), :],
                dst_v.at[pl.ds(al(((1 - zl) * 2 + kf) * 512 + half * 256, 256), 256), :],
                dst_s.at[half * 2 + kf], dst_r.at[half * 2 + kf],
                up // 2, n * 4 + (up % 2) * 2 + kf,
            ).wait_recv()

    my_st = st_r.at[n]

    def st_copy(g, d, at):
        ref = st_r.at[at, :, pl.ds(al(g * 512, 512), 512)]
        return send(
            ref, ref, st_ss.at[g * PLANE + d], st_rs.at[g * PLANE + at], r, plane(d) * 4 + zk
        )

    @pl.loop(0, 4)
    def _(turn):
        g = (x + jnp.where(turn < 2, turn, 5 - turn)) % 4

        @pl.when(turn > 0)
        def _():
            pass_on(g * 4 + y, 1, 0, x, y).wait_recv()

        for d in (1, 3, 2):
            slot = g * 4 + (y + d) % 4
            pass_on(slot, 0, 0, x, y).wait_recv()

            @pl.when(turn > 0)
            def _():
                pass_on(slot, 1, 0, x, y).wait_recv()

        for h in range(2):
            cols = pl.ds(al(g * 512 + h * 256, 256), 256)
            l = lax.dot_general(dst_v[...], src_v[cols, :], NT, preferred_element_type=F32)
            m = jnp.max(l, axis=0, keepdims=True)
            e = jnp.exp(l - m)
            p_v[:, cols] = e
            my_st[0:1, cols] = m
            my_st[1:2, cols] = jnp.sum(e, axis=0, keepdims=True)

        @pl.loop(1, PLANE)
        def _(d):
            st_copy(g, d, n).start()

    for half in range(2):
        send(
            state_ref.at[pl.ds(half * 256, 256), :],
            state_v.at[pl.ds(al((1 - zl) * 512 + half * 256, 256), 256), :],
            dst_s.at[5 + half], dst_r.at[5 + half],
            up // 2, n * 4 + (up % 2) * 2 + k,
        ).wait_recv()

    @pl.loop(1, 8)
    def _(d):
        vst_copy(d, lax.rem(me + d, 8)).wait_recv()

    @pl.loop(1, ROWS)
    def _(d):
        at = lax.rem(r + d, ROWS)
        tok_at = tok_v.at[pl.ds(al(at * 128, 128), 128), :]
        send(tok_at, tok_at, tok_s.at[d], tok_r.at[at], at, c).wait_recv()

    tokens = tok_v[0:128, :].astype(F32)
    for part in range(1, 4):
        tokens = tokens + tok_v[part * 128:(part + 1) * 128, :].astype(F32)
    tokens = tokens.astype(BF16)
    for low in range(2):
        vmax = vst_r[low * 4, 0:1, :]
        for part in range(1, 4):
            vmax = jnp.maximum(vmax, vst_r[low * 4 + part, 0:1, :])
        vsum = jnp.zeros((1, 512), F32)
        for part in range(4):
            at = low * 4 + part
            vsum = vsum + vst_r[at, 1:2, :] * jnp.exp(vst_r[at, 0:1, :] - vmax)
        norm = vmax + jnp.log(vsum)
        scores = lax.dot_general(
            tokens, state_v[low * 512:(low + 1) * 512, :], NT, preferred_element_type=F32
        )
        emit_v[:, low * 512:(low + 1) * 512] = jnp.exp(scores - norm)

    @pl.loop(0, 4)
    def _(g):
        @pl.loop(1, PLANE)
        def _(d):
            st_copy(g, d, plane(d)).wait_recv()

    @pl.loop(1, PLANE)
    def _(d):
        at = plane(d)
        sps = sp_v.at[pl.ds(al(at * B, B), B), :]
        send(sps, sps, sp_s.at[d], sp_r.at[at], r, at * 4 + zk).wait_recv()

    big = st_r[0, 0:1, :]
    for i in range(1, PLANE):
        big = jnp.maximum(big, st_r[i, 0:1, :])
    tot = jnp.zeros((1, NC), F32)
    for i in range(PLANE):
        tot = tot + st_r[i, 1:2, :] * jnp.exp(st_r[i, 0:1, :] - big)
    stat_v[0:1, :] = tot
    stat_v[1:2, :] = jnp.exp(my_st[0:1, :] - big)
    for i in range(PLANE):
        lanes = slice(i * BLK, (i + 1) * BLK)
        w_v[:, lanes] = (sp_v[i * B:(i + 1) * B, :].astype(F32) / stat_v[0:1, lanes]).astype(BF16)

    def pl_copy(t, d, at):
        ref = pl_r.at[t, at]
        return send(ref, ref, pl_ss.at[t, d], pl_rs.at[t, at], r, plane(d) * 4 + zk)

    def col_copy(t, d, at):
        to = column(d)
        ref = col_r.at[t, at]
        return send(ref, ref, col_ss.at[t, d], col_rs.at[t, at], to // 4, n * 4 + to % 4)

    def plane_start(t, part):
        both = jnp.concatenate([part, part], axis=0)
        pl_r[t, pl.ds(n, 1)] = jnp.sum(both.T, axis=0, keepdims=True)[None]

        @pl.loop(1, PLANE)
        def _(d):
            pl_copy(t, d, n).start()

    def plane_finish(t):
        @pl.loop(1, PLANE)
        def _(d):
            pl_copy(t, d, plane(d)).wait_recv()

        acc = pl_r[t, 0]
        for i in range(1, PLANE):
            acc = acc + pl_r[t, i]
        col_r[t, pl.ds(q, 1)] = acc[None]

        @pl.loop(1, PLANE)
        def _(d):
            col_copy(t, d, q).start()

    def column_finish(t):
        @pl.loop(1, PLANE)
        def _(d):
            col_copy(t, d, column(d)).wait_recv()

        acc = col_r[t, 0]
        for i in range(1, PLANE):
            acc = acc + col_r[t, i]
        return acc / S

    def step(t, first):
        def tile(j):
            rows = pl.ds(al(j * 256, 256), 256)
            if first:
                tr = (p_v[rows, :] * stat_v[1:2, :]).astype(BF16)
                t_v[rows, :] = tr
            else:
                tr = t_v[rows, :]
            return lax.dot_general(w_v[...], tr, NT, preferred_element_type=F32)

        peer = n * 4 + zl * 2 + (1 - k)

        @pl.loop(0, 4)
        def _(i):
            cs_s[t, i] = tile(((i // 2) * 2 + (1 - k)) * 2 + i % 2)
            send(cs_s.at[t, i], cs_r.at[t, i], cs_ss.at[t, i], cs_rs.at[t, i], r, peer).start()

        part_v[...] = jnp.zeros_like(part_v)

        @pl.loop(0, 4)
        def _(i):
            own = tile(((i // 2) * 2 + k) * 2 + i % 2)
            send(cs_s.at[t, i], cs_r.at[t, i], cs_ss.at[t, i], cs_rs.at[t, i], r, peer).wait_recv()
            own = own + cs_r[t, i]
            seen = own * emit_v[t * B:(t + 1) * B, pl.ds(al(i * 256, 256), 256)]
            part_v[...] += seen[:, 0:128] + seen[:, 128:256]
            for h in range(2):
                piece = i * 2 + h
                zs_s[t, piece] = own[:, h * 128:(h + 1) * 128]

                @pl.when(piece != me)
                def _():
                    send(
                        zs_s.at[t, piece], zs_r.at[t, me], zs_ss.at[t, piece], zs_rs.at[t, me],
                        piece % 4, n * 4 + (piece // 4) * 2 + k,
                    ).start()

        plane_start(t, part_v[...])
        plane_finish(t)
        acc_v[0:64, 0:128] = zs_s[t, me]

        @pl.loop(1, 8)
        def _(d):
            at = lax.rem(me + d, 8)
            send(
                zs_s.at[t, at], zs_r.at[t, at], zs_ss.at[t, at], zs_rs.at[t, at],
                at % 4, n * 4 + (at // 4) * 2 + k,
            ).wait_recv()
            acc_v[0:64, 0:128] += zs_r[t, at]

        return acc_v[0:64, 0:128] * emit_v[t * B:(t + 1) * B, pl.ds(al(me * 128, 128), 128)]

    joint = step(0, True)
    my_j = j_v.at[n]
    my_j[...] = joint

    @pl.loop(1, PLANE)
    def _(d):
        send(my_j, my_j, j_ss.at[d], j_rs.at[n], r, plane(d) * 4 + zk).start()

    scale1 = column_finish(0)
    ln_ref[...] = jnp.log(scale1)[:, 0:B]
    wide1 = jnp.broadcast_to(scale1, (128, 128)).T[0:64, :]

    @pl.loop(1, PLANE)
    def _(d):
        at = plane(d)
        send(my_j, j_v.at[at], j_ss.at[d], j_rs.at[at], r, at * 4 + zk).wait_recv()

    for i in range(PLANE):
        lanes = slice(i * BLK, (i + 1) * BLK)
        probs = (j_v[i] / wide1).astype(BF16).astype(F32)
        w_v[:, lanes] = (probs / stat_v[0:1, lanes]).astype(BF16)

    joint = step(1, False)
    my_fin = fin_v.at[r]
    my_fin[...] = joint

    @pl.loop(1, ROWS)
    def _(d):
        send(my_fin, my_fin, fin_ss.at[d], fin_rs.at[r], lax.rem(r + d, ROWS), c).start()

    scale2 = column_finish(1)
    ln_ref[...] += jnp.log(scale2)[:, 0:B]
    wide2 = jnp.broadcast_to(scale2, (128, 128)).T[0:64, :]

    @pl.loop(1, ROWS)
    def _(d):
        at = lax.rem(r + d, ROWS)
        send(my_fin, fin_v.at[at], fin_ss.at[d], fin_rs.at[at], at, c).wait_recv()

    for part in range(4):
        out_ref[:, part * 128:(part + 1) * 128] = fin_v[part] / wide2

    @pl.when(moved)
    def _():
        pi_src.wait_send()
        pi_sp.wait_send()

    dst_core.wait_send()
    for cpy in dst_copies:
        cpy.wait_send()

    for d in range(1, 4):
        for part in range(4):
            own_copy(part, d).wait_send()
        for e in range(1, 4):
            for half in range(2):
                forward(half, d, e).wait_send()

    @pl.loop(1, PLANE)
    def _(d):
        to = plane(d) * 4 + zk
        send(my_sp, my_sp, sp_s.at[d], sp_r.at[n], r, to).wait_send()
        for g in range(4):
            st_copy(g, d, n).wait_send()
        send(my_j, my_j, j_ss.at[d], j_rs.at[n], r, to).wait_send()
        for t in range(2):
            pl_copy(t, d, n).wait_send()
            col_copy(t, d, q).wait_send()

    @pl.loop(1, 8)
    def _(d):
        vst_copy(d, me).wait_send()

    @pl.loop(1, ROWS)
    def _(d):
        to = lax.rem(r + d, ROWS)
        send(tok_mine, tok_mine, tok_s.at[d], tok_r.at[r], to, c).wait_send()
        send(my_fin, my_fin, fin_ss.at[d], fin_rs.at[r], to, c).wait_send()

    peer = n * 4 + zl * 2 + (1 - k)
    for t in range(2):
        @pl.loop(0, 4)
        def _(i):
            send(cs_s.at[t, i], cs_r.at[t, i], cs_ss.at[t, i], cs_rs.at[t, i], r, peer).wait_send()

        @pl.loop(1, 8)
        def _(d):
            at = lax.rem(me + d, 8)
            send(
                zs_s.at[t, at], zs_r.at[t, me], zs_ss.at[t, at], zs_rs.at[t, me],
                at % 4, n * 4 + (at // 4) * 2 + k,
            ).wait_send()


def on_device(src_emb, dst_emb, state_emb, word_emb, start_probs, token_ids):
    vmem = pl.BlockSpec(memory_space=pltpu.VMEM)
    hbm = pl.BlockSpec(memory_space=pl.ANY)
    dma = pltpu.SemaphoreType.DMA
    V = pltpu.VMEM
    out, ln = pl.pallas_call(
        kernel,
        out_shape=(
            jax.ShapeDtypeStruct((B, 512), F32),
            jax.ShapeDtypeStruct((1, B), F32),
        ),
        in_specs=[vmem] + [hbm] * 5,
        out_specs=(vmem, vmem),
        scratch_shapes=[
            V((8000, E), BF16), V((1024, E), BF16), V((NC, E), BF16), V((NC, E), BF16),
            V((PLANE * B, BLK), BF16), V((NC, NC), F32), V((NC, NC), BF16), V((B, NC), BF16),
            V((512, E), BF16), V((128, E), F32), V((8, 2, 512), F32),
            V((PLANE, 2, NC), F32), V((2, NC), F32), V((128, 1024), F32), V((B, 128), F32),
            V((2, 4, B, 256), F32), V((2, 4, B, 256), F32), V((2, 8, B, 128), F32),
            V((2, 8, B, 128), F32), V((PLANE, B, BLK), F32), V((2, PLANE, 1, 128), F32),
            V((2, PLANE, 1, 128), F32), V((4, B, 128), F32),
            dma((5,)), dma((2,)), dma((2,)), dma((7,)), dma((7,)), dma((48,)), dma((32,)), dma((16,)),
            dma((16,)), dma((4,)), dma((4,)), dma((8,)), dma((8,)), dma((64,)), dma((64,)),
            dma((2, 4)), dma((2, 4)), dma((2, 8)), dma((2, 8)), dma((16,)), dma((16,)),
            dma((2, 16)), dma((2, 16)), dma((2, 16)), dma((2, 16)), dma((4,)), dma((4,)),
        ],
        compiler_params=pltpu.CompilerParams(
            collective_id=0, has_side_effects=True, vmem_limit_bytes=60 * 1024 * 1024
        ),
        name="forward",
    )(token_ids, src_emb, dst_emb, state_emb, word_emb, start_probs)
    return out, ln.reshape(B)


def solution(mesh):
    in_specs = (
        P(("row", "col"), None),
        P("col", None),
        P("col", None),
        P("row", None),
        P(None, "row"),
        P(),
    )
    out_specs = (P(None, "col"), P())
    return jax.shard_map(
        on_device, mesh=mesh, in_specs=in_specs, out_specs=out_specs, check_vma=False
    )
```

```python
import functools

import jax
import jax.numpy as jnp
from jax import lax
from jax.experimental import pallas as pl
from jax.experimental.pallas import tpu as pltpu
from jax.sharding import PartitionSpec as P

S = 32768
E = 256
B = 64
ROWS = 4
PLANE = 16
ZK = 4
NC = 2048
BLK = 128
WCH = 800
MESH = pl.DeviceIdType.MESH
F32 = jnp.float32
BF16 = jnp.bfloat16
NT = (((1,), (1,)), ((), ()))


def al(value, step):
    return pl.multiple_of(value, step)


def kernel(
    ids_ref, src_ref, dst_ref, state_ref, word_ref, sp_ref, out_ref, ln_ref,
    word_v, state_v, dst_v, src_v, sp_v, p_v, t_v, w_v, tok_v, acc_v, vst_r, st_r, stat_v,
    emit_v, part_v, ids_v, cs_s, cs_r, zs_s, zs_r, j_v, col_r, pl_r, fin_v,
    loc_sem, pi_s, pi_r, ag_r, cs_rs, out_sem, in_sem,
):
    r = lax.axis_index("row")
    c = lax.axis_index("col")
    n = c // 4
    x = n // 4
    y = n % 4
    zk = c % 4
    zl = zk // 2
    k = zk % 2
    q = r * 4 + zk

    def send(src, dst, ss, rs, row, col):
        return pltpu.make_async_remote_copy(
            src_ref=src, dst_ref=dst, send_sem=ss, recv_sem=rs,
            device_id=(row, col), device_id_type=MESH,
        )

    def arrived(ref, sem):
        send(ref, ref, out_sem.at[0], sem, r, c).wait_recv()

    def left(ref, sem):
        send(ref, ref, sem, in_sem.at[0], r, c).wait_send()

    def plane(d):
        return lax.rem(n + d, PLANE)

    def column(d):
        return lax.rem(q + d, PLANE)

    my_state = state_v.at[pl.ds(al(zl * 512, 512), 512), :]
    cp_ids = pltpu.make_async_copy(ids_ref, ids_v, loc_sem.at[5])
    cp_ids.start()
    cp_state = pltpu.make_async_copy(state_ref, my_state, loc_sem.at[0])
    cp_state.start()
    cp_word = pltpu.make_async_copy(word_ref, word_v, loc_sem.at[1])
    cp_word.start()
    cp_dst = pltpu.make_async_copy(dst_ref, dst_v.at[pl.ds(al(zk * 512, 512), 512), :], loc_sem.at[2])
    cp_dst.start()

    def owner(xc, yc, a, low, bit):
        g = (1 - (a + yc // 2) % 2) * 2 + bit
        return (xc + g) % 4, jnp.where(g == 2, 1 - low, low)

    rt, zt = owner(r, x, c % 16 // 8, c % 4 // 2, c % 2)
    ct = (r * 4 + x) * 4 + zt * 2 + c % 8 // 4
    g0 = (r + 4 - x) % 4
    a0 = (1 - g0 // 2 + y // 2) % 2
    low0 = jnp.where(g0 == 2, 1 - zl, zl)
    rf = x
    cf = y * 16 + a0 * 8 + k * 4 + low0 * 2 + g0 % 2
    moved = jnp.logical_or(rt != r, ct != c)

    barrier = pltpu.get_barrier_semaphore()

    @pl.loop(1, PLANE)
    def _(d):
        pl.semaphore_signal(barrier, inc=1, device_id=(r, plane(d) * 4 + zk), device_id_type=MESH)
        other = column(d)
        pl.semaphore_signal(
            barrier, inc=1, device_id=(other // 4, n * 4 + other % 4), device_id_type=MESH
        )

    @pl.when(moved)
    def _():
        pl.semaphore_signal(barrier, inc=1, device_id=(rt, ct), device_id_type=MESH)
        pl.semaphore_signal(barrier, inc=1, device_id=(rf, cf), device_id_type=MESH)

    cp_state.wait()
    cp_word.wait()
    acc_v[...] = jnp.zeros_like(acc_v)
    cp_ids.wait()
    row = ids_v[...].astype(F32)
    row = jnp.concatenate([row[0:1], row[1:2]], axis=1)
    emit_v[:, 0:128] = jnp.broadcast_to(row, (128, 128)).T
    base = r * 8000

    def vocab(i, carry):
        m, s = carry
        words = word_v[pl.ds(al(i * WCH, 16), WCH), :]
        l = lax.dot_general(words, my_state[...], NT, preferred_element_type=F32)
        m2 = jnp.maximum(m, jnp.max(l, axis=0, keepdims=True))
        s2 = s * jnp.exp(m - m2) + jnp.sum(jnp.exp(l - m2), axis=0, keepdims=True)
        at = lax.broadcasted_iota(jnp.int32, (128, WCH), 1) + (base + i * WCH)
        hot = jnp.where(emit_v[:, 0:1] == at.astype(F32), 1.0, 0.0).astype(BF16)
        acc_v[...] += jnp.dot(hot, words, preferred_element_type=F32)
        return m2, s2

    init = (jnp.full((1, 512), -jnp.inf, F32), jnp.zeros((1, 512), F32))
    carry = lax.fori_loop(0, 4, vocab, init)

    pl.semaphore_wait(barrier, jnp.where(moved, 32, 30))

    nt = ct // 4
    sp_mine = sp_ref.at[:, pl.ds(al(c * BLK, BLK), BLK)]
    my_rows = src_v.at[pl.ds(al(n * BLK, BLK), BLK), :]
    my_sp = sp_v.at[pl.ds(al(n * B, B), B), :]
    pi_src = send(src_ref, src_v.at[pl.ds(al(nt * BLK, BLK), BLK), :], pi_s.at[0], pi_r.at[0], rt, ct)
    pi_sp = send(sp_mine, sp_v.at[pl.ds(al(nt * B, B), B), :], pi_s.at[1], pi_r.at[1], rt, ct)

    @pl.when(moved)
    def _():
        pi_src.start()
        pi_sp.start()

    @pl.when(jnp.logical_not(moved))
    def _():
        a = pltpu.make_async_copy(src_ref, my_rows, loc_sem.at[3])
        b = pltpu.make_async_copy(sp_mine, my_sp, loc_sem.at[4])
        a.start()
        b.start()
        a.wait()
        b.wait()

    carry = lax.fori_loop(4, 7, vocab, carry)

    z = r * 2 + zl
    up = lax.rem(z + 1, 8)
    down = lax.rem(z + 7, 8)
    send(
        dst_ref, dst_v.at[pl.ds(al(zk * 512, 512), 512), :], out_sem.at[0], in_sem.at[0],
        r, n * 4 + zl * 2 + (1 - k),
    ).start()
    for half, to in ((0, up), (1, down)):
        for kt in range(2):
            send(
                dst_ref.at[pl.ds(half * 256, 256), :],
                dst_v.at[pl.ds(al(zk * 512 + half * 256, 256), 256), :],
                out_sem.at[0], in_sem.at[0], to // 2, n * 4 + (to % 2) * 2 + kt,
            ).start()

    @pl.when(moved)
    def _():
        send(src_ref, my_rows, pi_s.at[0], pi_r.at[0], rf, cf).wait_recv()
        send(sp_mine, my_sp, pi_s.at[1], pi_r.at[1], rf, cf).wait_recv()

    def half_of(slot, half):
        return src_v.at[pl.ds(al(slot * BLK + half * 64, 64), 64), :]

    def pass_on(slot, half, sem, xt, yt):
        ref = half_of(slot, half)
        return send(ref, ref, out_sem.at[1], ag_r.at[sem], r, (xt * 4 + yt) * 4 + zk)

    def own_copy(part, d):
        sem = (d, 4 + d, 8 + x, 8 + x)[part]
        if part in (0, 3):
            return pass_on(n, part % 2, sem, (x + d) % 4, y)
        return pass_on(n, part % 2, sem, x, (y + d) % 4)

    def forward(half, d, e):
        if half == 0:
            xd = (x + d) % 4
            return pass_on(xd * 4 + y, 0, 8 + xd, x, (y + e) % 4)
        return pass_on(x * 4 + (y + d) % 4, 1, 8 + x, (x + e) % 4, y)

    for part in range(4):
        for d in (1, 3, 2):
            own_copy(part, d).start()

    for half, to in ((0, up), (1, down)):
        send(
            state_ref.at[pl.ds(half * 256, 256), :],
            state_v.at[pl.ds(al(zl * 512 + half * 256, 256), 256), :],
            out_sem.at[0], in_sem.at[1], to // 2, n * 4 + (to % 2) * 2 + k,
        ).start()

    vm, vs = lax.fori_loop(7, 10, vocab, carry)

    me = zl * 4 + r
    my_vst = vst_r.at[me]
    my_vst[0:1, :] = vm
    my_vst[1:2, :] = vs
    tok_mine = tok_v.at[pl.ds(al(r * 128, 128), 128), :]
    tok_mine[...] = acc_v[...].astype(BF16)

    def vst_copy(d, at):
        to = lax.rem(me + d, 8)
        ref = vst_r.at[at]
        return send(
            ref, ref, out_sem.at[3], in_sem.at[3], to % 4, n * 4 + (to // 4) * 2 + k
        )

    for d in (1, 3, 2):
        pass_on((x + d) % 4 * 4 + y, 0, 4 - d, x, y).wait_recv()
        for e in (1, 3, 2):
            forward(0, d, e).start()
        pass_on(x * 4 + (y + d) % 4, 1, 8 - d, x, y).wait_recv()
        for e in (1, 3, 2):
            forward(1, d, e).start()

    @pl.loop(1, PLANE)
    def _(d):
        send(my_sp, my_sp, out_sem.at[2], in_sem.at[2], r, plane(d) * 4 + zk).start()

    @pl.loop(1, 8)
    def _(d):
        vst_copy(d, me).start()

    @pl.loop(1, ROWS)
    def _(d):
        send(tok_mine, tok_mine, out_sem.at[4], in_sem.at[4], lax.rem(r + d, ROWS), c).start()

    cp_dst.wait()
    arrived(dst_v.at[0:1536, :], in_sem.at[0])

    my_st = st_r.at[n]

    def st_copy(g, d, at):
        ref = st_r.at[at, :, pl.ds(al(g * 512, 512), 512)]
        return send(ref, ref, out_sem.at[5], in_sem.at[5], r, plane(d) * 4 + zk)

    @pl.loop(0, 4)
    def _(turn):
        g = (x + jnp.where(turn < 2, turn, 5 - turn)) % 4

        @pl.when(turn == 0)
        def _():
            arrived(src_v.at[0:192, :], ag_r.at[8 + g])

        @pl.when(turn > 0)
        def _():
            arrived(src_v.at[0:448, :], ag_r.at[8 + g])

        for h in range(2):
            cols = pl.ds(al(g * 512 + h * 256, 256), 256)
            l = lax.dot_general(dst_v[...], src_v[cols, :], NT, preferred_element_type=F32)
            m = jnp.max(l, axis=0, keepdims=True)
            e = jnp.exp(l - m)
            p_v[:, cols] = e
            my_st[0:1, cols] = m
            my_st[1:2, cols] = jnp.sum(e, axis=0, keepdims=True)

        @pl.loop(1, PLANE)
        def _(d):
            st_copy(g, d, n).start()

    arrived(state_v.at[0:512, :], in_sem.at[1])

    arrived(vst_r.at[0:7], in_sem.at[3])
    arrived(tok_v.at[0:384, :], in_sem.at[4])

    tokens = tok_v[0:128, :].astype(F32)
    for part in range(1, 4):
        tokens = tokens + tok_v[part * 128:(part + 1) * 128, :].astype(F32)
    tokens = tokens.astype(BF16)
    for low in range(2):
        vmax = vst_r[low * 4, 0:1, :]
        for part in range(1, 4):
            vmax = jnp.maximum(vmax, vst_r[low * 4 + part, 0:1, :])
        vsum = jnp.zeros((1, 512), F32)
        for part in range(4):
            at = low * 4 + part
            vsum = vsum + vst_r[at, 1:2, :] * jnp.exp(vst_r[at, 0:1, :] - vmax)
        norm = vmax + jnp.log(vsum)
        scores = lax.dot_general(
            tokens, state_v[low * 512:(low + 1) * 512, :], NT, preferred_element_type=F32
        )
        emit_v[:, low * 512:(low + 1) * 512] = jnp.exp(scores - norm)

    arrived(st_r.at[0:15], in_sem.at[5])

    arrived(sp_v.at[0:15 * B, :], in_sem.at[2])

    big = st_r[0, 0:1, :]
    for i in range(1, PLANE):
        big = jnp.maximum(big, st_r[i, 0:1, :])
    tot = jnp.zeros((1, NC), F32)
    for i in range(PLANE):
        tot = tot + st_r[i, 1:2, :] * jnp.exp(st_r[i, 0:1, :] - big)
    stat_v[0:1, :] = tot
    stat_v[1:2, :] = jnp.exp(my_st[0:1, :] - big)
    for i in range(PLANE):
        lanes = slice(i * BLK, (i + 1) * BLK)
        w_v[:, lanes] = (sp_v[i * B:(i + 1) * B, :].astype(F32) / stat_v[0:1, lanes]).astype(BF16)

    def pl_copy(t, d, at):
        ref = pl_r.at[t, at]
        return send(ref, ref, out_sem.at[6 + t], in_sem.at[6 + t], r, plane(d) * 4 + zk)

    def col_copy(t, d, at):
        to = column(d)
        ref = col_r.at[t, at]
        return send(ref, ref, out_sem.at[8 + t], in_sem.at[8 + t], to // 4, n * 4 + to % 4)

    def plane_start(t, part):
        both = jnp.concatenate([part, part], axis=0)
        pl_r[t, pl.ds(n, 1)] = jnp.sum(both.T, axis=0, keepdims=True)[None]

        @pl.loop(1, PLANE)
        def _(d):
            pl_copy(t, d, n).start()

    def plane_finish(t):
        arrived(pl_r.at[t, 0:15], in_sem.at[6 + t])

        acc = pl_r[t, 0]
        for i in range(1, PLANE):
            acc = acc + pl_r[t, i]
        col_r[t, pl.ds(q, 1)] = acc[None]

        @pl.loop(1, PLANE)
        def _(d):
            col_copy(t, d, q).start()

    def column_finish(t):
        arrived(col_r.at[t, 0:15], in_sem.at[8 + t])

        acc = col_r[t, 0]
        for i in range(1, PLANE):
            acc = acc + col_r[t, i]
        return acc / S

    def step(t, forward_half):
        peer = n * 4 + zl * 2 + (1 - k)
        if t == 0:
            mine = a0 * 4 + low0 * 2 + g0 % 2
        else:
            mine = zl * 4 + r

        def order(j):
            if t == 0:
                far = jnp.where(j < 2, 1 - a0, a0)
                near = jnp.where(j % 2 == 0, 1 - low0, low0)
            else:
                near = jnp.where(j < 2, 1 - r // 2, r // 2)
                far = jnp.where(j % 2 == 0, 1 - zl, zl)
            return far, near

        def target(far, near, bit):
            if t == 0:
                return owner(x, y, far, near, bit)
            return near * 2 + bit, far

        def tile(j):
            rows = pl.ds(al(j * 256, 256), 256)
            if t == 0:
                tr = (p_v[rows, :] * stat_v[1:2, :]).astype(BF16)
                t_v[rows, :] = tr
            else:
                tr = t_v[rows, :]
            return lax.dot_general(w_v[...], tr, NT, preferred_element_type=F32)

        def cs_copy(i):
            return send(cs_s.at[t, i], cs_r.at[t, i], out_sem.at[10 + t], cs_rs.at[t, i], r, peer)

        def peer_tile(j):
            far, near = order(j)
            i = far * 2 + near
            cs_s[t, i] = tile((far * 2 + (1 - k)) * 2 + near)
            cs_copy(i).start()

        def piece_copy(half, far, near, bit):
            piece = far * 4 + near * 2 + bit
            row, low = target(far, near, bit)
            lines = pl.ds(half * 32, 32)
            return piece, send(
                zs_s.at[t, piece, lines], zs_r.at[t, me, lines], out_sem.at[12 + t],
                in_sem.at[10 + t * 2 + half], row, n * 4 + low * 2 + k,
            )

        def pieces(half, j, act):
            far, near = order(j)
            for bit in range(2):
                piece = far * 4 + near * 2 + bit

                @pl.when(piece != mine)
                def _():
                    act(piece_copy(half, far, near, bit)[1])

        part_v[...] = jnp.zeros_like(part_v)
        @pl.loop(0, 4)
        def _(j):
            peer_tile(j)

        @pl.loop(0, 4)
        def _(j):
            far, near = order(j)
            i = far * 2 + near
            own = tile((far * 2 + k) * 2 + near)
            cs_copy(i).wait_recv()
            own = own + cs_r[t, i]
            seen = own * emit_v[t * B:(t + 1) * B, pl.ds(al(i * 256, 256), 256)]
            part_v[...] += seen[:, 0:128] + seen[:, 128:256]
            for bit in range(2):
                zs_s[t, i * 2 + bit] = own[:, bit * 128:(bit + 1) * 128]
            pieces(0, j, lambda cpy: cpy.start())

        @pl.loop(0, 4)
        def _(j):
            pieces(1, j, lambda cpy: cpy.start())

        plane_start(t, part_v[...])
        for half in range(2):
            lines = slice(half * 32, (half + 1) * 32)
            arrived(zs_r.at[t, 0:7, lines], in_sem.at[10 + t * 2 + half])
            acc = zs_s[t, mine, lines]
            for d in range(1, 8):
                acc = acc + zs_r[t, lax.rem(me + d, 8), lines]
            lows = slice(t * B + half * 32, t * B + (half + 1) * 32)
            forward_half(half, acc * emit_v[lows, pl.ds(al(mine * 128, 128), 128)])
            if half == 0:
                plane_finish(t)

        def drain():
            left(cs_s.at[t], out_sem.at[10 + t])
            left(zs_s.at[t, 0:7], out_sem.at[12 + t])

        return drain

    def j_copy(half, d, at):
        ref = j_v.at[at, pl.ds(half * 32, 32)]
        return send(ref, ref, out_sem.at[14], in_sem.at[14], r, plane(d) * 4 + zk)

    def share(half, joint):
        j_v[n, half * 32:(half + 1) * 32] = joint

        @pl.loop(1, PLANE)
        def _(d):
            j_copy(half, d, n).start()

    drain0 = step(0, share)
    scale1 = column_finish(0)
    ln_ref[...] = jnp.log(scale1)[:, 0:B]
    wide1 = jnp.broadcast_to(scale1, (128, 128)).T[0:64, :]

    arrived(j_v.at[0:15], in_sem.at[14])

    for i in range(PLANE):
        lanes = slice(i * BLK, (i + 1) * BLK)
        probs = (j_v[i] / wide1).astype(BF16).astype(F32)
        w_v[:, lanes] = (probs / stat_v[0:1, lanes]).astype(BF16)

    def fin_copy(half, d, at):
        ref = fin_v.at[at, pl.ds(half * 32, 32)]
        return send(
            ref, ref, out_sem.at[15], in_sem.at[15], lax.rem(r + d, ROWS), c
        )

    def finish(half, joint):
        fin_v[r, half * 32:(half + 1) * 32] = joint

        @pl.loop(1, ROWS)
        def _(d):
            fin_copy(half, d, r).start()

    drain1 = step(1, finish)
    scale2 = column_finish(1)
    ln_ref[...] += jnp.log(scale2)[:, 0:B]
    wide2 = jnp.broadcast_to(scale2, (128, 128)).T[0:64, :]

    arrived(fin_v.at[0:3], in_sem.at[15])

    for part in range(4):
        out_ref[:, part * 128:(part + 1) * 128] = fin_v[part] / wide2

    @pl.when(moved)
    def _():
        pi_src.wait_send()
        pi_sp.wait_send()

    left(dst_v.at[0:2048, :], out_sem.at[0])
    left(src_v.at[0:1920, :], out_sem.at[1])
    left(sp_v.at[0:15 * B, :], out_sem.at[2])
    left(vst_r.at[0:7], out_sem.at[3])
    left(tok_v.at[0:384, :], out_sem.at[4])
    left(st_r.at[0:15], out_sem.at[5])
    for t in range(2):
        left(pl_r.at[t, 0:15], out_sem.at[6 + t])
        left(col_r.at[t, 0:15], out_sem.at[8 + t])
    left(j_v.at[0:15], out_sem.at[14])
    left(fin_v.at[0:3], out_sem.at[15])
    drain0()
    drain1()


def hand_over(out_ref, ln_ref, out_to, ln_to):
    out_to[...] = out_ref[...]
    ln_to[...] = ln_ref[...]


def on_device(src_emb, dst_emb, state_emb, word_emb, start_probs, token_ids):
    vmem = pl.BlockSpec(memory_space=pltpu.VMEM)
    hbm = pl.BlockSpec(memory_space=pl.ANY)
    dma = pltpu.SemaphoreType.DMA
    V = pltpu.VMEM
    out, ln = pl.pallas_call(
        kernel,
        out_shape=(
            jax.ShapeDtypeStruct((B, 512), F32),
            jax.ShapeDtypeStruct((1, B), F32),
        ),
        in_specs=[hbm] * 6,
        out_specs=(vmem, vmem),
        scratch_shapes=[
            V((8000, E), BF16), V((1024, E), BF16), V((NC, E), BF16), V((NC, E), BF16),
            V((PLANE * B, BLK), BF16), V((NC, NC), F32), V((NC, NC), BF16), V((B, NC), BF16),
            V((512, E), BF16), V((128, E), F32), V((8, 2, 512), F32),
            V((PLANE, 2, NC), F32), V((2, NC), F32), V((128, 1024), F32), V((B, 128), F32), V((2, B), jnp.int32),
            V((2, 4, B, 256), F32), V((2, 4, B, 256), F32), V((2, 8, B, 128), F32),
            V((2, 8, B, 128), F32), V((PLANE, B, BLK), F32), V((2, PLANE, 1, 128), F32),
            V((2, PLANE, 1, 128), F32), V((4, B, 128), F32),
            dma((6,)), dma((2,)), dma((2,)), dma((12,)), dma((2, 4)), dma((16,)), dma((16,)),
        ],
        compiler_params=pltpu.CompilerParams(
            collective_id=0, has_side_effects=True, vmem_limit_bytes=60 * 1024 * 1024
        ),
        name="forward",
    )(token_ids.T, src_emb, dst_emb, state_emb, word_emb, start_probs)
    out, ln = pl.pallas_call(
        hand_over,
        out_shape=(
            jax.ShapeDtypeStruct((B, 512), F32),
            jax.ShapeDtypeStruct((1, B), F32),
        ),
        in_specs=(vmem, vmem),
        out_specs=(vmem, vmem),
        name="hand_over",
    )(out, ln)
    return out, ln.reshape(B)


def solution(mesh):
    in_specs = (
        P(("row", "col"), None),
        P("col", None),
        P("col", None),
        P("row", None),
        P(None, "row"),
        P(),
    )
    out_specs = (P(None, "col"), P())
    return jax.shard_map(
        on_device, mesh=mesh, in_specs=in_specs, out_specs=out_specs, check_vma=False
    )
```
